768 devices in a mesh: slab: 12 (over z_lo, core), row: 64 (over x, y, z_hi).
Axes of the slice: x: 4, y: 8, z: 12 (z_hi: 2, z_lo: 6; z = z_hi * 6 + z_lo), core: 2. Of those that a mesh axis runs over, the one named last changes fastest.
Arguments:
- velocity: bfloat16 [512, 96, 3, 1536], P('row', 'slab'), may hold values from -6 to 6
- deriv_x: bfloat16 [1536, 1536], replicated, may hold values from -0.15625 to 0.15625
- deriv_y: bfloat16 [512, 512], replicated, may hold values from -0.25 to 0.25
- metric_x: float32 [1536], replicated, may hold values from 0.5 to 2
- metric_y: float32 [512], replicated, may hold values from 0.5 to 2
- coarse_force: bfloat16 [128, 48, 3, 192], P('row', 'slab'), may hold values from -6 to 6
- row_map: int32 [512], P('row'), may hold values from 0 to 127, as said below
- x_index: int32 [1536], replicated, may hold values from 0 to 190, as said below
- x_weight: bfloat16 [1536], replicated, may hold values from 0 to 1
Outputs:
- tendency: bfloat16 [512, 96, 3, 1536], P('row', 'slab')
- updated: bfloat16 [512, 96, 3, 1536], P('row', 'slab')
The draws below stay inside these ranges and needn't reach their ends.
Inputs may be any that keep to these rules, and one draw needn't show every extreme that they name: `row_map`: each coarse row is named by exactly 4 fine rows. `x_index`: every value of the range is named by some fine column.
All inputs are finite; a program needn't handle non-finite values.
Results may differ from the reference program's by a relative error of at most 0.004.
Values may be sent and summed in bfloat16 or wider, within the bound.
A program may use at most 32 MiB of HBM per device.

```python
import math
import jax
import jax.numpy as jnp
from jax import lax

NX = 1536
NY = 512
NYC = 128
NXC = 192
NZ = 96
NZC = 48


def draw_row_map(key, part):
    order = jax.random.permutation(jax.random.fold_in(key, 11), NY)
    return (order % NYC).astype(jnp.int32)


def draw_x_index(key, part):
    order = jax.random.permutation(jax.random.fold_in(key, 23), NX)
    return (order % (NXC - 1)).astype(jnp.int32)


def block_scale(stream_key, extent, pieces, smallest, top_value):
    gain = 1.0
    for axis_at, shards_of in pieces:
        heights = jax.random.uniform(jax.random.fold_in(jax.random.fold_in(stream_key, 6), axis_at), (shards_of,), jnp.float32, smallest / len(pieces), top_value / len(pieces))
        gain = gain * jnp.repeat(jnp.exp(heights), extent[axis_at] // shards_of).reshape((-1,) + (1,) * (len(extent) - 1 - axis_at))
    return gain


def gaussian(own_key, shape, deviation, bound, pieces=(), held_as=jnp.bfloat16):
    loudness = block_scale(own_key, shape, pieces, -0.22, 0.18) if pieces else 1.0
    values = jax.random.normal(own_key, shape, jnp.float32) * deviation * loudness
    return jnp.minimum(jnp.maximum(values, -bound), bound).astype(held_as)


def setup_inputs(seed: int = 0) -> dict:
    streams_of = jax.random.split(jax.random.key(seed), 10)
    return {
        "velocity": gaussian(streams_of[0], (NY, NZ, 3, NX), 1.0, 6.0, ((0, 64), (1, 12))),
        "deriv_x": gaussian(streams_of[1], (NX, NX), NX ** -0.5, 0.15625),
        "deriv_y": gaussian(streams_of[2], (NY, NY), NY ** -0.5, 0.25),
        "metric_x": jnp.clip(jnp.exp(jax.random.uniform(streams_of[3], (NX,), jnp.float32, math.log(0.5), math.log(2.0))), 0.5, 2.0),
        "metric_y": jnp.clip(jnp.exp(jax.random.uniform(streams_of[4], (NY,), jnp.float32, math.log(0.5), math.log(2.0))), 0.5, 2.0),
        "coarse_force": gaussian(streams_of[5], (NYC, NZC, 3, NXC), 1.0, 6.0, ((0, 64), (1, 12))),
        "row_map": draw_row_map(jax.random.fold_in(streams_of[9], 71), 0),
        "x_index": draw_x_index(jax.random.fold_in(streams_of[9], 71), 0),
        "x_weight": jnp.clip(jax.random.uniform(streams_of[8], (NX,), jnp.float32, 0.0, 1.0), 0.0, 1.0).astype(jnp.bfloat16),
    }


rk_weight = 0.5


def refine_levels(extended):
    lower = extended[:, :-1]
    middle = (0.5 * (lower.astype(jnp.float32) + extended[:, 1:].astype(jnp.float32))).astype(jnp.bfloat16)
    stacked = jnp.stack([lower, middle], axis=2)
    return stacked.reshape(extended.shape[0], 2 * (extended.shape[1] - 1), extended.shape[2], extended.shape[3])


def upsample_table(x_index, x_weight, coarse_width):
    positions = jnp.arange(coarse_width, dtype=jnp.int32)[:, None]
    nothing = jnp.zeros((), jnp.bfloat16)
    left_part = jnp.where(positions == x_index[None, :], x_weight[None, :], nothing)
    right_weight = (1.0 - x_weight.astype(jnp.float32)).astype(jnp.bfloat16)
    right_part = jnp.where(positions == x_index[None, :] + 1, right_weight[None, :], nothing)
    return left_part + right_part


def reference(velocity, deriv_x, deriv_y, metric_x, metric_y, coarse_force, row_map, x_index, x_weight):
    table = upsample_table(x_index, x_weight, NXC)
    extended = jnp.concatenate([coarse_force, coarse_force[:, -1:]], axis=1)
    force_levels = refine_levels(extended)
    levels_first = jnp.transpose(force_levels, (1, 0, 2, 3))
    velocity_first = jnp.transpose(velocity, (1, 0, 2, 3))

    def one_level(inputs):
        plane, coarse_plane = inputs
        along_x = jnp.dot(plane.reshape(NY * 3, NX), deriv_x, preferred_element_type=jnp.float32).reshape(NY, 3, NX) * metric_x
        along_y = (jnp.dot(deriv_y, plane.reshape(NY, 3 * NX), preferred_element_type=jnp.float32) * metric_y[:, None]).astype(jnp.bfloat16).reshape(NY, 3, NX)
        chosen = jnp.take(coarse_plane, row_map, axis=0)
        forcing = jnp.dot(chosen.reshape(NY * 3, NXC), table, preferred_element_type=jnp.float32).reshape(NY, 3, NX)
        moving = plane.astype(jnp.float32)
        result = forcing - (moving[:, 0:1] * along_x + moving[:, 1:2] * along_y.astype(jnp.float32))
        return result.astype(jnp.bfloat16), (moving + rk_weight * result).astype(jnp.bfloat16)

    tendency, updated = lax.map(one_level, (velocity_first, levels_first))
    return jnp.transpose(tendency, (1, 0, 2, 3)), jnp.transpose(updated, (1, 0, 2, 3))
```

```python
import jax
import jax.numpy as jnp
from jax import lax
from jax.experimental import pallas as pl
from jax.experimental.pallas import tpu as pltpu
from jax.sharding import PartitionSpec as P

rk_weight = 0.5
MESH = pl.DeviceIdType.MESH
F32 = jnp.float32
BF16 = jnp.bfloat16

NXD, NYD = 4, 8
LANES = 128
WIDE = NXD * LANES
PIECES = 9
FORCE = PIECES


def kernel(
    v_ref, coarse_ref, rowmap_ref, dy_ref, my_ref, mx_ref, xi_ref, xw_ref, dx_hbm,
    tend_ref, upd_ref,
    dx, ybuf, xbuf, fx, fz, zbuf, rxbuf, rybuf, rim, rm_y, rm_x, ax, chosen, table, forcing,
    send, recv, dx_sem,
):
    slab = lax.axis_index("slab")
    row = lax.axis_index("row")
    slabs = lax.axis_size("slab")
    zhi = row % 2
    y = (row // 2) % NYD
    x = row // (2 * NYD)

    def at(xx, yy, zz):
        return (slab, (xx * NYD + yy) * 2 + zz)

    y_peers = [(lax.rem(y + i, NYD), at(x, lax.rem(y + i, NYD), zhi)) for i in range(1, NYD)]
    x_peers = [(lax.rem(x + i, NXD), at(lax.rem(x + i, NXD), y, zhi)) for i in range(1, NXD)]
    z_peer = at(x, y, 1 - zhi)
    below = (lax.rem(slab + slabs - 1, slabs), row)
    above = (lax.rem(slab + 1, slabs), row)

    dx_copy = pltpu.make_async_copy(dx_hbm, dx, dx_sem)
    dx_copy.start()

    barrier = pltpu.get_barrier_semaphore()
    greeted = [d for _, d in y_peers] + [d for _, d in x_peers] + [z_peer, below, above]
    for device in greeted:
        pl.semaphore_signal(barrier, inc=1, device_id=device, device_id_type=MESH)
    pl.semaphore_wait(barrier, len(greeted))

    def remote(src, dst, stage, k, device):
        pltpu.make_async_remote_copy(
            src_ref=src, dst_ref=dst, send_sem=send.at[stage, k], recv_sem=recv.at[stage, k],
            device_id=device, device_id_type=MESH,
        ).start()

    def local(src, dst, stage, k):
        pltpu.make_async_copy(src, dst, recv.at[stage, k]).start()

    def wait_for(sem, part):
        pltpu.make_async_copy(part, part, sem).wait()

    def quarter(i):
        return pl.ds(pl.multiple_of(i * LANES, LANES), LANES)

    def eighth(i):
        return pl.ds(pl.multiple_of(i * NYD, NYD), NYD)

    def start_y(k, src):
        for j, device in y_peers:
            remote(src.at[j], ybuf.at[k, y], 0, k, device)
        local(src.at[y], ybuf.at[k, y], 0, k)

    def start_x(k, dst):
        wait_for(recv.at[0, k], ybuf.at[k])
        for i, device in x_peers:
            remote(ybuf.at[k, :, :, quarter(i)], dst.at[eighth(x)], 1, k, device)
        local(ybuf.at[k, :, :, quarter(x)], dst.at[eighth(x)], 1, k)

    def start_z(k):
        wait_for(recv.at[1, k], xbuf.at[k, :, zhi])
        remote(xbuf.at[k, :, zhi], xbuf.at[k, :, zhi], 2, k, z_peer)

    def start_back_x(k):
        for i, device in x_peers:
            remote(zbuf.at[k, eighth(i)], rxbuf.at[k, :, :, quarter(x)], 3, k, device)
        local(zbuf.at[k, eighth(x)], rxbuf.at[k, :, :, quarter(x)], 3, k)

    def start_back_y(k):
        wait_for(recv.at[3, k], rxbuf.at[k])
        for j, device in y_peers:
            remote(rxbuf.at[k, j], rybuf.at[k, y], 4, k, device)
        local(rxbuf.at[k, y], rybuf.at[k, y], 4, k)

    def wait_back_y(k):
        wait_for(recv.at[4, k], rybuf.at[k])

    start_y(0, v_ref.at[0])
    start_y(FORCE, coarse_ref)
    for _, device in y_peers:
        remote(rowmap_ref, rm_y.at[y], 5, 0, device)
    local(rowmap_ref, rm_y.at[y], 5, 0)
    start_y(1, v_ref.at[1])
    start_y(2, v_ref.at[2])

    spot = lax.broadcasted_iota(jnp.int32, (NXD * NYD * 8, 512), 0)
    here = lax.broadcasted_iota(jnp.int32, (NXD * NYD * 8, 512), 1)
    mine = (spot // 8) * 16 + zhi * 8 + spot % 8
    metric = jnp.sum(jnp.where(here == mine, my_ref[...], 0.0), axis=1, keepdims=True)

    start_x(0, xbuf.at[0, :, zhi])
    start_x(FORCE, fx)
    wait_for(recv.at[5, 0], rm_y)
    for _, device in x_peers:
        remote(rm_y, rm_x.at[eighth(x)], 5, 1, device)
    local(rm_y, rm_x.at[eighth(x)], 5, 1)
    start_z(0)

    wait_for(recv.at[1, FORCE], fx)
    pack_to = lax.broadcasted_iota(jnp.int32, (64, 256), 0)
    pack_from = lax.broadcasted_iota(jnp.int32, (64, 256), 1)
    pack = (pack_from == (pack_to // 2) * 8 + pack_to % 2).astype(F32).astype(BF16)
    packed = jnp.dot(pack, fx[...].reshape(256, LANES), preferred_element_type=F32)
    fz[zhi] = packed.astype(BF16)
    remote(fz.at[zhi], fz.at[zhi], 2, FORCE, z_peer)

    def forward(k, _):
        @pl.when(k + 2 < PIECES)
        def _():
            start_y(k + 2, v_ref.at[k + 2])

        start_x(k, xbuf.at[k, :, zhi])

        @pl.when(k > 1)
        def _():
            start_z(k - 1)

        return 0

    lax.fori_loop(1, PIECES, forward, 0)
    start_z(PIECES - 1)

    dx_copy.wait()

    def along_x(n, _):
        cols = pl.ds(pl.multiple_of(n * 256, 256), 256)
        total = jnp.zeros((192, 256), F32)
        for q in range(3):
            lhs = v_ref[3 * q : 3 * q + 3].reshape(192, WIDE)
            total += jnp.dot(lhs, dx[q * WIDE : (q + 1) * WIDE, cols], preferred_element_type=F32)
        ax[:, cols] = total * mx_ref[:, cols]
        return 0

    lax.fori_loop(0, 6, along_x, 0)

    wait_for(recv.at[2, FORCE], fz.at[1 - zhi])
    wait_for(recv.at[5, 1], rm_x)
    named = rm_x[...].reshape(256, LANES).astype(F32)
    lane = lax.broadcasted_iota(jnp.int32, (256, LANES), 1)
    coarse_row = ((lane % 64) // 2) * 4 + (lane // 64) * 2 + lane % 2
    choice = (named == coarse_row.astype(F32)).astype(F32).astype(BF16)
    picked = jnp.dot(choice, fz[...].reshape(LANES, LANES), preferred_element_type=F32)
    zbuf[FORCE] = picked.astype(BF16).reshape(NXD * NYD, 8, LANES)
    start_back_x(FORCE)

    cell = lax.broadcasted_iota(jnp.int32, (256, WIDE), 0)
    for q in range(3):
        cols = slice(q * WIDE, (q + 1) * WIDE)
        left = xw_ref[:, cols]
        right = (1.0 - left).astype(BF16).astype(F32)
        index = xi_ref[:, cols]
        table[:, cols] = (
            jnp.where(cell == index, left, 0.0) + jnp.where(cell == index + 1, right, 0.0)
        ).astype(BF16)

    start_back_y(FORCE)

    def turn(k):
        wait_for(recv.at[2, k], xbuf.at[k, :, 1 - zhi])
        slope = jnp.dot(
            dy_ref[:, zhi].reshape(256, 512), xbuf[k].reshape(512, LANES),
            preferred_element_type=F32,
        )
        zbuf[k] = (slope * metric).astype(BF16).reshape(NXD * NYD, 8, LANES)
        start_back_x(k)

    turn(0)
    wait_back_y(FORCE)
    remote(rybuf.at[FORCE, 0:2], rim, 5, 2, below)
    turn(1)
    start_back_y(0)

    wait_for(recv.at[5, 2], rim)
    topmost = slab == slabs - 1
    for c in range(3):
        cols = slice(c * LANES, (c + 1) * LANES)
        for h in range(2):
            levels = [rybuf[FORCE, 2 * m + h, :, cols].astype(F32) for m in range(4)]
            levels.append(jnp.where(topmost, levels[3], rim[h, :, cols].astype(F32)))
            for m in range(4):
                out = slice(h * LANES, (h + 1) * LANES)
                chosen[c * 8 + 2 * m, :, out] = levels[m].astype(BF16)
                chosen[c * 8 + 2 * m + 1, :, out] = (0.5 * (levels[m] + levels[m + 1])).astype(BF16)

    def upsample(n, _):
        cols = pl.ds(pl.multiple_of(n * 256, 256), 256)
        forcing[:, cols] = jnp.dot(
            chosen[...].reshape(192, 256), table[:, cols], preferred_element_type=F32
        )
        return 0

    lax.fori_loop(0, 6, upsample, 0)

    def finish(q):
        u = v_ref[3 * q].astype(F32).reshape(64, WIDE)
        v = v_ref[3 * q + 1].astype(F32).reshape(64, WIDE)
        for c in range(3):
            k = 3 * q + c
            wait_back_y(k)
            rows = slice(64 * c, 64 * c + 64)
            cols = slice(q * WIDE, (q + 1) * WIDE)
            along_y = rybuf[k].astype(F32).reshape(64, WIDE)
            own = v_ref[k].astype(F32).reshape(64, WIDE)
            t = forcing[rows, cols] - (u * ax[rows, cols] + v * along_y)
            tend_ref[k] = t.astype(BF16).reshape(8, 8, WIDE)
            upd_ref[k] = (own + rk_weight * t).astype(BF16).reshape(8, 8, WIDE)

    for k in range(2, PIECES):
        turn(k)
        start_back_y(k - 1)
        if k == 4:
            finish(0)
        if k == 7:
            finish(1)
    start_back_y(PIECES - 1)

    def sent(k, _):
        wait_for(send.at[0, k], ybuf.at[k, 0 : NYD - 1])
        wait_for(send.at[1, k], xbuf.at[0, 0 : 8 * (NXD - 1), 0])
        wait_for(send.at[3, k], xbuf.at[0, 0 : 8 * (NXD - 1), 0])
        return 0

    lax.fori_loop(0, PIECES + 1, sent, 0)

    def sent_z(k, _):
        wait_for(send.at[2, k], xbuf.at[k, :, zhi])
        return 0

    lax.fori_loop(0, PIECES, sent_z, 0)
    wait_for(send.at[2, FORCE], fz.at[zhi])
    wait_for(send.at[5, 0], rm_y.at[0 : NYD - 1])
    wait_for(send.at[5, 1], rm_x.at[0 : 8 * (NXD - 1)])
    wait_for(send.at[5, 2], rim)

    finish(2)

    def sent_y(k, _):
        wait_for(send.at[4, k], rybuf.at[k, 0 : NYD - 1])
        return 0

    lax.fori_loop(0, PIECES + 1, sent_y, 0)


def shards(
    velocity, deriv_x, deriv_y, metric_x, metric_y, coarse_force, row_map, x_index, x_weight
):
    rows, levels, components, width = velocity.shape
    pieces = velocity.reshape(rows, levels, components, 3, WIDE).transpose(3, 2, 1, 0, 4)
    pieces = pieces.reshape(PIECES, levels, rows, WIDE)
    coarse = jnp.pad(coarse_force, ((0, 6), (0, 0), (0, 1), (0, 64)))
    coarse = coarse.reshape(8, 4, 4, 2, LANES).transpose(1, 3, 0, 2, 4).reshape(8, 8, WIDE)
    named = jnp.broadcast_to(row_map.astype(F32).astype(BF16)[:, None], (8, LANES))
    vmem = pl.BlockSpec(memory_space=pltpu.VMEM)
    out = jax.ShapeDtypeStruct((PIECES, 8, 8, WIDE), BF16)
    tend, upd = pl.pallas_call(
        kernel,
        out_shape=(out, out),
        in_specs=[vmem] * 8 + [pl.BlockSpec(memory_space=pltpu.HBM)],
        out_specs=(vmem, vmem),
        scratch_shapes=[
            pltpu.VMEM((width, width), BF16),
            pltpu.VMEM((PIECES + 1, 8, 8, WIDE), BF16),
            pltpu.VMEM((PIECES, 32, 2, 8, LANES), BF16),
            pltpu.VMEM((32, 8, LANES), BF16),
            pltpu.VMEM((2, 64, LANES), BF16),
            pltpu.VMEM((PIECES + 1, 32, 8, LANES), BF16),
            pltpu.VMEM((PIECES + 1, 8, 8, WIDE), BF16),
            pltpu.VMEM((PIECES + 1, 8, 8, WIDE), BF16),
            pltpu.VMEM((2, 8, WIDE), BF16),
            pltpu.VMEM((8, 8, LANES), BF16),
            pltpu.VMEM((32, 8, LANES), BF16),
            pltpu.VMEM((192, width), F32),
            pltpu.VMEM((24, 8, 256), BF16),
            pltpu.VMEM((256, width), BF16),
            pltpu.VMEM((192, width), F32),
            pltpu.SemaphoreType.DMA((6, PIECES + 1)),
            pltpu.SemaphoreType.DMA((6, PIECES + 1)),
            pltpu.SemaphoreType.DMA,
        ],
        compiler_params=pltpu.CompilerParams(
            collective_id=0, has_side_effects=True, vmem_limit_bytes=48 << 20
        ),
    )(
        pieces,
        coarse,
        named,
        deriv_y.reshape(32, 2, 8, 512),
        metric_y.reshape(1, -1),
        metric_x.reshape(1, -1),
        x_index.reshape(1, -1),
        x_weight.astype(F32).reshape(1, -1),
        deriv_x,
    )

    def natural(a):
        a = a.reshape(3, components, levels, rows, WIDE).transpose(3, 2, 1, 0, 4)
        return a.reshape(velocity.shape)

    return natural(tend), natural(upd)


def solution(mesh):
    return jax.shard_map(
        shards,
        mesh=mesh,
        in_specs=(
            P("row", "slab", None, None), P(), P(), P(), P(),
            P("row", "slab", None, None), P("row"), P(), P(),
        ),
        out_specs=(P("row", "slab", None, None), P("row", "slab", None, None)),
        check_vma=False,
    )
```

```python
import jax
import jax.numpy as jnp
from jax import lax
from jax.experimental import pallas as pl
from jax.experimental.pallas import tpu as pltpu
from jax.sharding import PartitionSpec as P

rk_weight = 0.5
MESH = pl.DeviceIdType.MESH
F32 = jnp.float32
BF16 = jnp.bfloat16

NXD, NYD = 4, 8
LANES = 128
WIDE = NXD * LANES
PIECES = 9
FORCE = PIECES
EXTRA = FORCE + 1
MID, REST = (0, 2), (2, 5)
FIRST = (5, 7)
LAST = (7, 9)


def kernel(
    v_hbm, coarse_ref, const_ref, dy_hbm, dx_hbm,
    tend_ref, upd_ref,
    v_ref, dy_ref, dx, xbuf, fx, fz, zbuf, fback, rybuf, zfirst, zlast, rim,
    ax, chosen, table, forcing,
    send, recv, load_sem,
):
    slab = lax.axis_index("slab")
    row = lax.axis_index("row")
    slabs = lax.axis_size("slab")
    zhi = row % 2
    y = (row // 2) % NYD
    x = row // (2 * NYD)
    place = x * NYD + y

    plane = []
    for i in range(NXD):
        for j in range(NYD):
            if i or j:
                px, py = lax.rem(x + i, NXD), lax.rem(y + j, NYD)
                plane.append((px, py, (slab, (px * NYD + py) * 2 + zhi)))
    z_peer = (slab, place * 2 + 1 - zhi)
    below = (lax.rem(slab + slabs - 1, slabs), row)
    above = (lax.rem(slab + 1, slabs), row)

    barrier = pltpu.get_barrier_semaphore()
    greeted = [device for _, _, device in plane] + [z_peer, below, above]
    for device in greeted:
        pl.semaphore_signal(barrier, inc=1, device_id=device, device_id_type=MESH)

    loads = [
        pltpu.make_async_copy(v_hbm, v_ref, load_sem.at[0]),
        pltpu.make_async_copy(dy_hbm, dy_ref, load_sem.at[1]),
        pltpu.make_async_copy(dx_hbm, dx, load_sem.at[2]),
    ]
    for load in loads:
        load.start()
    pl.semaphore_wait(barrier, len(greeted))

    left = []

    def remote(src, dst, stage, slot, device):
        pltpu.make_async_remote_copy(
            src_ref=src, dst_ref=dst, send_sem=send.at[stage, slot], recv_sem=recv.at[stage, slot],
            device_id=device, device_id_type=MESH,
        ).start()

    def local(src, dst, stage, slot):
        pltpu.make_async_copy(src, dst, recv.at[stage, slot]).start()

    def wait_for(sem, part):
        pltpu.make_async_copy(part, part, sem).wait()

    def quarter(i):
        return pl.ds(pl.multiple_of(i * LANES, LANES), LANES)

    def span(group):
        return slice(*group)

    def out(slot, src, dst, count):
        for i, j, device in plane:
            remote(src.at[:, j, :, quarter(i)], dst.at[:, place], 0, slot, device)
        local(src.at[:, y, :, quarter(x)], dst.at[:, place], 0, slot)
        left.append((0, slot, zbuf.at[0:count, 0:31]))

    def wait_out(slot, dst):
        wait_for(recv.at[0, slot], dst)

    def cross(slot, src, dst):
        remote(src, dst, 1, slot, z_peer)
        left.append((1, slot, dst))

    def wait_cross(slot, dst):
        wait_for(recv.at[1, slot], dst)

    def back(slot, src, dst, count):
        for i, j, device in plane:
            remote(src.at[:, i * NYD + j], dst.at[:, y, :, quarter(x)], 2, slot, device)
        local(src.at[:, place], dst.at[:, y, :, quarter(x)], 2, slot)
        left.append((2, slot, zbuf.at[0:count, 0:31]))

    def wait_back(slot, dst):
        wait_for(recv.at[2, slot], dst)

    def half(group, side):
        return xbuf.at[span(group), :, side]

    cross(2, v_hbm.at[span(FIRST)], zfirst)
    out(0, v_hbm.at[span(MID)], half(MID, zhi), 2)
    out(4, coarse_ref, fx, 1)
    out(1, v_hbm.at[span(REST)], half(REST, zhi), 3)
    out(3, v_hbm.at[span(LAST)], half(LAST, zhi), 2)

    block = lax.broadcasted_iota(jnp.int32, (32, 8, 512), 0)
    inner = lax.broadcasted_iota(jnp.int32, (32, 8, 512), 1)
    lane = lax.broadcasted_iota(jnp.int32, (32, 8, 512), 2)
    y_metric = const_ref[3:4, 0:512].reshape(1, 1, 512)
    metric = [
        jnp.sum(
            jnp.where(lane == block * 16 + inner + side * 8, y_metric, 0.0), axis=2, keepdims=True
        )
        for side in (zhi, 1 - zhi)
    ]
    pack_to = lax.broadcasted_iota(jnp.int32, (64, 256), 0)
    pack_from = lax.broadcasted_iota(jnp.int32, (64, 256), 1)
    pack = (pack_from == (pack_to >> 1) * 8 + (pack_to & 1)).astype(F32).astype(BF16)
    for k in range(*LAST):
        xbuf[k, :, 1 - zhi] = jnp.zeros((32, 8, LANES), BF16)

    wait_out(0, half(MID, zhi))
    cross(0, half(MID, zhi), half(MID, zhi))

    wait_out(4, fx)
    packed = jnp.dot(pack, fx[0].reshape(256, LANES), preferred_element_type=F32)
    fz[zhi] = packed.astype(BF16)
    cross(4, fz.at[zhi], fz.at[zhi])

    wait_out(1, half(REST, zhi))
    cross(1, half(REST, zhi), half(REST, zhi))

    wait_cross(2, zfirst)
    out(5, zfirst, half(FIRST, 1 - zhi), 2)
    out(2, v_hbm.at[span(FIRST)], half(FIRST, zhi), 2)

    for load in loads:
        load.wait()

    def along_x(n):
        cols = slice(n * 256, (n + 1) * 256)
        total = jnp.zeros((192, 256), F32)
        for q in range(3):
            lhs = v_ref[3 * q : 3 * q + 3].reshape(192, WIDE)
            total += jnp.dot(lhs, dx[q * WIDE : (q + 1) * WIDE, cols], preferred_element_type=F32)
        ax[:, cols] = total * const_ref[0:1, cols]

    def slope(k, half):
        out = jnp.dot(
            dy_ref[:, zhi if half == 0 else 1 - zhi].reshape(256, 512),
            xbuf[k].reshape(512, LANES),
            preferred_element_type=F32,
        )
        return (out.reshape(32, 8, LANES) * metric[half]).astype(BF16)

    def fill_table(q):
        cell = lax.broadcasted_iota(jnp.int32, (256, WIDE), 0).astype(F32)
        cols = slice(q * WIDE, (q + 1) * WIDE)
        weight = const_ref[2:3, cols]
        rest = (1.0 - weight).astype(BF16).astype(F32)
        index = const_ref[1:2, cols]
        table[:, cols] = (
            jnp.where(cell == index, weight, 0.0) + jnp.where(cell == index + 1.0, rest, 0.0)
        ).astype(BF16)

    def turn(group):
        for k in range(*group):
            zbuf[k] = slope(k, 0)

    wait_out(3, half(LAST, zhi))
    for b, k in enumerate(range(*LAST)):
        zbuf[EXTRA + b] = slope(k, 1)
    back(6, zbuf.at[EXTRA : EXTRA + 2], rybuf.at[EXTRA - 1 : EXTRA + 1], 2)
    turn(LAST)
    back(3, zbuf.at[span(LAST)], rybuf.at[span(LAST)], 2)

    wait_cross(4, fz.at[1 - zhi])
    lane = lax.broadcasted_iota(jnp.int32, (32, 8, LANES), 2)
    inner = lax.broadcasted_iota(jnp.int32, (32, 8, LANES), 1)
    named = fx[0].astype(F32)[:, 2:3, :]
    named = jnp.sum(jnp.where(lane == inner, named, 0.0), axis=2, keepdims=True)
    coarse_row = ((lane & 63) >> 1) * 4 + (lane >> 6) * 2 + (lane & 1)
    choice = jnp.where(named == coarse_row.astype(F32), 1.0, 0.0).reshape(256, LANES).astype(BF16)
    picked = jnp.dot(choice, fz[...].reshape(LANES, LANES), preferred_element_type=F32)
    zbuf[FORCE] = picked.reshape(32, 8, LANES).astype(BF16)
    back(4, zbuf.at[FORCE:EXTRA], fback, 1)

    wait_back(6, rybuf.at[EXTRA - 1 : EXTRA + 1])
    cross(3, rybuf.at[EXTRA - 1 : EXTRA + 1], zlast)

    wait_out(5, half(FIRST, 1 - zhi))
    wait_out(2, half(FIRST, zhi))
    turn(FIRST)
    back(2, zbuf.at[span(FIRST)], rybuf.at[span(FIRST)], 2)

    wait_back(4, fback)
    remote(fback.at[0, 0:2], rim, 3, 0, below)
    left.append((3, 0, rim))

    wait_cross(0, half(MID, 1 - zhi))
    turn(MID)
    back(0, zbuf.at[span(MID)], rybuf.at[span(MID)], 2)

    def refine():
        wait_for(recv.at[3, 0], rim)
        topmost = slab == slabs - 1
        for c in range(3):
            cols = slice(c * LANES, (c + 1) * LANES)
            for h in range(2):
                levels = [fback[0, 2 * m + h, :, cols].astype(F32) for m in range(4)]
                levels.append(jnp.where(topmost, levels[3], rim[h, :, cols].astype(F32)))
                for m in range(4):
                    to = slice(h * LANES, (h + 1) * LANES)
                    chosen[c * 8 + 2 * m, :, to] = levels[m].astype(BF16)
                    half_way = 0.5 * (levels[m] + levels[m + 1])
                    chosen[c * 8 + 2 * m + 1, :, to] = half_way.astype(BF16)

    def upsample(n):
        cols = slice(n * 256, (n + 1) * 256)
        forcing[:, cols] = jnp.dot(
            chosen[...].reshape(192, 256), table[:, cols], preferred_element_type=F32
        )

    def finish(k):
        q, c = k // 3, k % 3
        rows = slice(64 * c, 64 * c + 64)
        cols = slice(q * WIDE, (q + 1) * WIDE)
        u = v_ref[3 * q].astype(F32).reshape(64, WIDE)
        v = v_ref[3 * q + 1].astype(F32).reshape(64, WIDE)
        along_y = rybuf[k].astype(F32).reshape(64, WIDE)
        if k >= LAST[0]:
            along_y += zlast[k - LAST[0]].astype(F32).reshape(64, WIDE)
            along_y = along_y.astype(BF16).astype(F32)
        here = v_ref[k].astype(F32).reshape(64, WIDE)
        t = forcing[rows, cols] - (u * ax[rows, cols] + v * along_y)
        tend_ref[k] = t.astype(BF16).reshape(8, 8, WIDE)
        upd_ref[k] = (here + rk_weight * t).astype(BF16).reshape(8, 8, WIDE)

    for q in range(3):
        fill_table(q)
    refine()
    for n in range(6):
        along_x(n)
        upsample(n)

    wait_cross(1, half(REST, 1 - zhi))
    turn(REST)
    back(1, zbuf.at[span(REST)], rybuf.at[span(REST)], 3)

    wait_back(0, rybuf.at[span(MID)])
    wait_back(2, rybuf.at[span(FIRST)])
    wait_back(3, rybuf.at[span(LAST)])
    for k in (*range(*MID), *range(*FIRST)):
        finish(k)
    for stage, slot, part in left:
        if (stage, slot) not in ((1, 3), (2, 1)):
            wait_for(send.at[stage, slot], part)
    wait_back(1, rybuf.at[span(REST)])
    for k in range(*REST):
        finish(k)
    wait_cross(3, zlast)
    for k in range(*LAST):
        finish(k)
    for stage, slot, part in left:
        if (stage, slot) in ((1, 3), (2, 1)):
            wait_for(send.at[stage, slot], part)


def shards(
    velocity, deriv_x, deriv_y, metric_x, metric_y, coarse_force, row_map, x_index, x_weight
):
    rows, levels, components, width = velocity.shape
    pieces = velocity.reshape(rows, levels, components, 3, WIDE).transpose(3, 2, 1, 0, 4)
    pieces = pieces.reshape(PIECES, levels, rows, WIDE)
    coarse = jnp.pad(coarse_force, ((0, 6), (0, 0), (0, 1), (0, 64)))
    coarse = coarse.reshape(8, 4, 4, 2, LANES).transpose(1, 3, 0, 2, 4).reshape(8, 8, WIDE)
    named = jnp.tile(jnp.pad(row_map.astype(F32), (0, LANES - rows)), 4)[None, None, :]
    third_row = lax.broadcasted_iota(jnp.int32, (8, 8, WIDE), 1) == 2
    coarse = jnp.where(third_row, named, coarse.astype(F32)).astype(BF16)[None]
    width_row = jnp.stack(
        [metric_x, x_index.astype(F32), x_weight.astype(F32), jnp.pad(metric_y, (0, width - 512))]
    )
    vmem = pl.BlockSpec(memory_space=pltpu.VMEM)
    hbm = pl.BlockSpec(memory_space=pltpu.HBM)
    out = jax.ShapeDtypeStruct((PIECES, 8, 8, WIDE), BF16)
    tend, upd = pl.pallas_call(
        kernel,
        out_shape=(out, out),
        in_specs=[hbm, vmem, vmem, hbm, hbm],
        out_specs=(vmem, vmem),
        scratch_shapes=[
            pltpu.VMEM((PIECES, 8, 8, WIDE), BF16),
            pltpu.VMEM((32, 2, 8, 512), BF16),
            pltpu.VMEM((width, width), BF16),
            pltpu.VMEM((PIECES, 32, 2, 8, LANES), BF16),
            pltpu.VMEM((1, 32, 8, LANES), BF16),
            pltpu.VMEM((2, 64, LANES), BF16),
            pltpu.VMEM((EXTRA + 2, 32, 8, LANES), BF16),
            pltpu.VMEM((1, 8, 8, WIDE), BF16),
            pltpu.VMEM((PIECES + 2, 8, 8, WIDE), BF16),
            pltpu.VMEM((2, 8, 8, WIDE), BF16),
            pltpu.VMEM((2, 8, 8, WIDE), BF16),
            pltpu.VMEM((2, 8, WIDE), BF16),
            pltpu.VMEM((192, width), F32),
            pltpu.VMEM((24, 8, 256), BF16),
            pltpu.VMEM((256, width), BF16),
            pltpu.VMEM((192, width), F32),
            pltpu.SemaphoreType.DMA((4, 8)),
            pltpu.SemaphoreType.DMA((4, 8)),
            pltpu.SemaphoreType.DMA((3,)),
        ],
        compiler_params=pltpu.CompilerParams(
            collective_id=0, has_side_effects=True, vmem_limit_bytes=48 << 20
        ),
    )(pieces, coarse, width_row, deriv_y.reshape(32, 2, 8, 512), deriv_x)

    def natural(a):
        a = a.reshape(3, components, levels, rows, WIDE).transpose(3, 2, 1, 0, 4)
        return a.reshape(velocity.shape)

    return natural(tend), natural(upd)


def solution(mesh):
    return jax.shard_map(
        shards,
        mesh=mesh,
        in_specs=(
            P("row", "slab", None, None), P(), P(), P(), P(),
            P("row", "slab", None, None), P("row"), P(), P(),
        ),
        out_specs=(P("row", "slab", None, None), P("row", "slab", None, None)),
        check_vma=False,
    )
```
